32 devices in a mesh: grp: 2 (over y), shard: 16 (over z, x, core).
Axes of the slice: x: 2, y: 2, z: 4, core: 2. Of those that a mesh axis runs over, the one named last changes fastest.
Arguments:
- projections: bfloat16 [3, 4096, 512], P(None, ('grp', 'shard')), may hold values from -6 to 6
- short_taps: float32 [3, 7, 512], replicated, may hold values from -2 to 2
- long_filter: float32 [4096, 512], P(('grp', 'shard')), may hold values from -0.09375 to 0.09375
- skip_gain: float32 [512], replicated, may hold values from 0.5 to 1.5
Outputs:
- output: bfloat16 [4096, 512], P(('grp', 'shard'))
The draws below stay inside these ranges and needn't reach their ends.
All inputs are finite; a program needn't handle non-finite values.
Results may differ from the reference program's by a relative error of at most 0.001.
Values may be sent and summed in bfloat16 or wider, within the bound.
A program may use at most 64 MiB of HBM per device.

```python
import jax
import jax.numpy as jnp
from jax import lax

CH = 512
WIDTH = 7
SEQ = 4096


def block_scale(key, dims, shards, smallest, top_value):
    level = 1.0
    for position, parts in shards:
        heights = jax.random.uniform(jax.random.fold_in(jax.random.fold_in(key, 6), position), (parts,), jnp.float32, smallest / len(shards), top_value / len(shards))
        level = level * jnp.repeat(jnp.exp(heights), dims[position] // parts).reshape((-1,) + (1,) * (len(dims) - 1 - position))
    return level


def bell_draw(rng, shape, scale, limit, split=(), held_as=jnp.bfloat16):
    gain = block_scale(rng, shape, split, -0.22, 0.18) if split else 1.0
    drawn = jax.random.normal(rng, shape, jnp.float32) * scale * gain
    return jnp.minimum(jnp.maximum(drawn, -limit), limit).astype(held_as)


def setup_inputs(seed: int = 0) -> dict:
    streams_of = jax.random.split(jax.random.key(seed), 5)
    projections = bell_draw(streams_of[0], (3, SEQ, CH), 1.0, 6.0, ((1, 32),))
    short_taps = bell_draw(streams_of[1], (3, WIDTH, CH), WIDTH ** -0.5, 2.0, (), jnp.float32)
    long_filter = bell_draw(streams_of[2], (SEQ, CH), SEQ ** -0.5, 0.09375, ((0, 32),), jnp.float32)
    skip_gain = jnp.clip(jax.random.uniform(streams_of[3], (CH,), jnp.float32, 0.5, 1.5), 0.5, 1.5)
    return {"projections": projections, "short_taps": short_taps, "long_filter": long_filter, "skip_gain": skip_gain}


def reference(projections, short_taps, long_filter, skip_gain):
    widened = projections.astype(jnp.float32)
    padded = jnp.pad(widened, ((0, 0), (WIDTH - 1, 0), (0, 0)))
    shortened = short_taps[:, 0, None, :] * padded[:, WIDTH - 1:WIDTH - 1 + SEQ, :]
    for tap_index in range(1, WIDTH):
        shortened = shortened + short_taps[:, tap_index, None, :] * padded[:, WIDTH - 1 - tap_index:WIDTH - 1 - tap_index + SEQ, :]
    query = shortened[0]
    mixed = shortened[1] * shortened[2]
    band_width = min(CH, 64)

    def one_band(pair):
        mixed_band, filt_band = pair
        zeros_band = jnp.zeros_like(mixed_band)
        mixed_spec = jnp.fft.fft(jnp.concatenate([mixed_band, zeros_band], axis=0), axis=0)
        filt_spec = jnp.fft.fft(jnp.concatenate([filt_band, zeros_band], axis=0), axis=0)
        back = jnp.fft.ifft(mixed_spec * filt_spec, axis=0)
        return jnp.real(back)[:SEQ].astype(mixed_band.dtype)

    mixed_bands = mixed.reshape(SEQ, CH // band_width, band_width).transpose(1, 0, 2)
    filt_bands = long_filter.reshape(SEQ, CH // band_width, band_width).transpose(1, 0, 2)
    conv = lax.map(one_band, (mixed_bands, filt_bands)).transpose(1, 0, 2).reshape(SEQ, CH)
    return (query * (conv + skip_gain * mixed)).astype(jnp.bfloat16)
```

```python
import functools
import math

import jax
import jax.numpy as jnp
import numpy as np
from jax import lax
from jax.experimental import pallas as pl
from jax.experimental.pallas import tpu as pltpu
from jax.sharding import PartitionSpec as P

precise = lax.Precision.HIGHEST


def from_behind(block, axis, distance):
    devices = range(lax.axis_size(axis))
    route = [(i - distance, i) for i in devices if i - distance in devices]
    return lax.ppermute(block, axis, route)


def angles_of(first, second, modulus):
    return (first * second % modulus).astype(jnp.float32) * (2.0 * math.pi / modulus)


def per_device(projections, short_taps, long_filter, skip_gain):
    positions = projections.shape[1]
    channels = projections.shape[2]
    taps_count = short_taps.shape[1]
    groups = lax.axis_size("grp")
    shards = lax.axis_size("shard")
    devices = groups * shards
    span_len = 2 * devices
    length = span_len * positions
    slice_len = positions * channels // devices
    device_id = lax.axis_index("grp") * shards + lax.axis_index("shard")
    rim_rows = from_behind(projections[:, positions - (taps_count - 1) :, :], ("grp", "shard"), 1)
    extended = jnp.concatenate([rim_rows, projections], axis=1)
    shortened = short_taps[:, 0, None, :] * extended[
        :, taps_count - 1 : taps_count - 1 + positions, :
    ].astype(jnp.float32)
    for tap_index in range(1, taps_count):
        shortened = shortened + short_taps[:, tap_index, None, :] * extended[
            :, taps_count - 1 - tap_index : taps_count - 1 - tap_index + positions, :
        ].astype(jnp.float32)
    query = shortened[0]
    mixed = shortened[1] * shortened[2]
    mixed_rows = mixed.reshape(groups, shards, slice_len)
    filt_rows = long_filter.reshape(groups, shards, slice_len)
    got_mixed, got_filt = (
        lax.all_to_all(
            lax.all_to_all(mixed_rows, "grp", split_axis=0, concat_axis=0, tiled=True),
            "shard",
            split_axis=1,
            concat_axis=1,
            tiled=True,
        ),
        lax.all_to_all(
            lax.all_to_all(filt_rows, "grp", split_axis=0, concat_axis=0, tiled=True),
            "shard",
            split_axis=1,
            concat_axis=1,
            tiled=True,
        ),
    )
    dev_ids = jnp.arange(devices, dtype=jnp.int32)
    freq_ids = jnp.arange(span_len, dtype=jnp.int32)
    outer = angles_of(freq_ids[:, None], dev_ids[None, :], span_len)
    outer_cos, outer_sin = (jnp.cos(outer), jnp.sin(outer))
    flat_ids = device_id * slice_len + jnp.arange(slice_len, dtype=jnp.int32)
    row_of = flat_ids // channels
    twist = angles_of(freq_ids[:, None], row_of[None, :], length)
    twist_cos, twist_sin = (jnp.cos(twist), jnp.sin(twist))

    def forward_outer(values):
        flat_values = values.reshape(devices, slice_len)
        real = jnp.dot(outer_cos, flat_values, precision=precise)
        imag = -jnp.dot(outer_sin, flat_values, precision=precise)
        turned_re = real * twist_cos + imag * twist_sin
        turned_im = imag * twist_cos - real * twist_sin
        return (
            turned_re.reshape(2, groups, shards, slice_len),
            turned_im.reshape(2, groups, shards, slice_len),
        )

    mixed_re, mixed_im = forward_outer(got_mixed)
    filt_re, filt_im = forward_outer(got_filt)
    mixed_re, mixed_im, filt_re, filt_im = (
        lax.all_to_all(
            lax.all_to_all(mixed_re, "grp", split_axis=1, concat_axis=1, tiled=True),
            "shard",
            split_axis=2,
            concat_axis=2,
            tiled=True,
        ),
        lax.all_to_all(
            lax.all_to_all(mixed_im, "grp", split_axis=1, concat_axis=1, tiled=True),
            "shard",
            split_axis=2,
            concat_axis=2,
            tiled=True,
        ),
        lax.all_to_all(
            lax.all_to_all(filt_re, "grp", split_axis=1, concat_axis=1, tiled=True),
            "shard",
            split_axis=2,
            concat_axis=2,
            tiled=True,
        ),
        lax.all_to_all(
            lax.all_to_all(filt_im, "grp", split_axis=1, concat_axis=1, tiled=True),
            "shard",
            split_axis=2,
            concat_axis=2,
            tiled=True,
        ),
    )
    row_ids = jnp.arange(positions, dtype=jnp.int32)
    inner = angles_of(row_ids[:, None], row_ids[None, :], positions)
    inner_cos, inner_sin = (jnp.cos(inner), jnp.sin(inner))

    def forward_inner(real, imag):
        real = real.reshape(2, positions, channels)
        imag = imag.reshape(2, positions, channels)
        out_re = jnp.einsum("kp,rpc->rkc", inner_cos, real, precision=precise) + jnp.einsum(
            "kp,rpc->rkc", inner_sin, imag, precision=precise
        )
        out_im = jnp.einsum("kp,rpc->rkc", inner_cos, imag, precision=precise) - jnp.einsum(
            "kp,rpc->rkc", inner_sin, real, precision=precise
        )
        return (out_re, out_im)

    spec_mixed_re, spec_mixed_im = forward_inner(mixed_re, mixed_im)
    spec_filt_re, spec_filt_im = forward_inner(filt_re, filt_im)
    prod_re = spec_mixed_re * spec_filt_re - spec_mixed_im * spec_filt_im
    prod_im = spec_mixed_re * spec_filt_im + spec_mixed_im * spec_filt_re
    back_re = jnp.einsum("kp,rkc->rpc", inner_cos, prod_re, precision=precise) - jnp.einsum(
        "kp,rkc->rpc", inner_sin, prod_im, precision=precise
    )
    back_im = jnp.einsum("kp,rkc->rpc", inner_cos, prod_im, precision=precise) + jnp.einsum(
        "kp,rkc->rpc", inner_sin, prod_re, precision=precise
    )
    own_freqs = jnp.arange(2, dtype=jnp.int32) * devices + device_id
    back_twist = angles_of(own_freqs[:, None], row_ids[None, :], length)
    back_cos, back_sin = (jnp.cos(back_twist)[:, :, None], jnp.sin(back_twist)[:, :, None])
    rot_re = (back_re * back_cos - back_im * back_sin).reshape(2, groups, shards, slice_len)
    rot_im = (back_re * back_sin + back_im * back_cos).reshape(2, groups, shards, slice_len)
    rot_re, rot_im = (
        lax.all_to_all(
            lax.all_to_all(rot_re, "grp", split_axis=1, concat_axis=1, tiled=True),
            "shard",
            split_axis=2,
            concat_axis=2,
            tiled=True,
        ),
        lax.all_to_all(
            lax.all_to_all(rot_im, "grp", split_axis=1, concat_axis=1, tiled=True),
            "shard",
            split_axis=2,
            concat_axis=2,
            tiled=True,
        ),
    )
    rot_re = rot_re.reshape(span_len, slice_len)
    rot_im = rot_im.reshape(span_len, slice_len)
    values = (
        jnp.einsum("kd,kf->df", outer_cos, rot_re, precision=precise)
        - jnp.einsum("kd,kf->df", outer_sin, rot_im, precision=precise)
    ) / length
    values = values.reshape(groups, shards, slice_len)
    conv_rows = lax.all_to_all(
        lax.all_to_all(values, "grp", split_axis=0, concat_axis=0, tiled=True),
        "shard",
        split_axis=1,
        concat_axis=1,
        tiled=True,
    )
    conv = conv_rows.reshape(positions, channels)
    return (query * (conv + skip_gain * mixed)).astype(jnp.bfloat16)


MESH = pl.DeviceIdType.MESH
LANES = 128
SUB = 8
HALO = 16


def turned(value, numerator, denominator):
    numerator %= denominator
    real, imag = value
    eighths, rest = divmod(8 * numerator, denominator)
    if rest == 0:
        half = math.sqrt(0.5)
        if eighths == 0:
            return (real, imag)
        if eighths == 2:
            return (-imag, real)
        if eighths == 4:
            return (-real, -imag)
        if eighths == 6:
            return (imag, -real)
        if eighths == 1:
            return ((real - imag) * half, (real + imag) * half)
        if eighths == 3:
            return ((real + imag) * -half, (real - imag) * half)
        if eighths == 5:
            return ((imag - real) * half, (real + imag) * -half)
        return ((real + imag) * half, (imag - real) * half)
    angle = 2.0 * math.pi * numerator / denominator
    cos, sin = (math.cos(angle), math.sin(angle))
    return (real * cos - imag * sin, real * sin + imag * cos)


def fft(loads, sign):
    count = len(loads)
    if count == 1:
        return [loads[0]()]
    even, odd = (fft(loads[::2], sign), fft(loads[1::2], sign))
    low, high = ([], [])
    for k in range(count // 2):
        moved = turned(odd[k], sign * k, count)
        low.append((even[k][0] + moved[0], even[k][1] + moved[1]))
        high.append((even[k][0] - moved[0], even[k][1] - moved[1]))
    return low + high


def dot3(values, table_hi, table_lo):
    hi = values.astype(jnp.bfloat16)
    lo = (values - hi.astype(jnp.float32)).astype(jnp.bfloat16)
    dot = functools.partial(jnp.dot, preferred_element_type=jnp.float32)
    return dot(hi, table_hi[...]) + (dot(lo, table_hi[...]) + dot(hi, table_lo[...]))


def owner_kernel(
    sizes,
    proj_ref,
    taps_ref,
    filt_ref,
    gain_ref,
    fwd_hi,
    fwd_lo,
    inv_hi,
    inv_lo,
    twist_cos,
    twist_sin,
    out_ref,
    rim,
    ext,
    query,
    direct,
    filt_out,
    mix_out,
    filt_in,
    mix_in,
    conv_out,
    conv_in,
    spec_a,
    spec_h,
    spec_g,
    rim_sems,
    send_sems,
    recv_sems,
):
    groups, shards, positions, channels, taps = sizes
    devices = groups * shards
    owned = channels // devices
    halves = owned // SUB
    per_chunk = LANES // owned
    chunks = channels // LANES
    me = lax.axis_index("grp") * shards + lax.axis_index("shard")

    def place(target):
        return (target // shards, target % shards)

    barrier = pltpu.get_barrier_semaphore()

    @pl.loop(1, devices)
    def _(step):
        pl.semaphore_signal(
            barrier, inc=1, device_id=place(lax.rem(me + step, devices)), device_id_type=MESH
        )

    def scatter_rows(chunk, turned_block, store):
        for part in range(per_chunk):
            for half in range(halves):
                first = part * owned + half * SUB
                store[half, chunk * per_chunk + part] = turned_block[first : first + SUB, :]

    for chunk in range(chunks):
        lanes = slice(chunk * LANES, (chunk + 1) * LANES)
        scatter_rows(chunk, filt_ref[:, lanes].T, filt_out)
        for which in range(3):
            ext[which, chunk, HALO:, :] = proj_ref[which, :, lanes].astype(jnp.float32)

    pl.semaphore_wait(barrier, devices - 1)

    rim_copy = pltpu.make_async_remote_copy(
        src_ref=proj_ref.at[:, positions - HALO :, :],
        dst_ref=rim,
        send_sem=rim_sems.at[0],
        recv_sem=rim_sems.at[1],
        device_id=place(lax.rem(me + 1, devices)),
        device_id_type=MESH,
    )
    rim_copy.start()

    def send_all(source, landing, kind, half):
        @pl.loop(1, devices)
        def _(step):
            target = lax.rem(me + step, devices)
            pltpu.make_async_remote_copy(
                src_ref=source.at[half, target],
                dst_ref=landing.at[half, me],
                send_sem=send_sems.at[kind, half],
                recv_sem=recv_sems.at[kind, half],
                device_id=place(target),
                device_id_type=MESH,
            ).start()

        landing[half, me] = source[half, me]

    def wait_all(landing, sems, kind, half):
        others = landing.at[half, pl.ds(0, devices - 1)]
        pltpu.make_async_copy(others, others, sems.at[kind, half]).wait()

    for half in range(halves):
        send_all(filt_out, filt_in, 0, half)

    rim_copy.wait()
    keep = jnp.where(me > 0, 1.0, 0.0).astype(jnp.float32)
    for chunk in range(chunks):
        lanes = slice(chunk * LANES, (chunk + 1) * LANES)
        for which in range(3):
            ext[which, chunk, :HALO, :] = rim[which, :, lanes].astype(jnp.float32) * keep

    def shortened(which, chunk):
        lanes = slice(chunk * LANES, (chunk + 1) * LANES)
        total = None
        for tap in range(taps):
            term = taps_ref[which, tap : tap + 1, lanes] * ext[
                which, chunk, HALO - tap : HALO - tap + positions, :
            ]
            total = term if total is None else total + term
        return total

    for chunk in range(chunks):
        mixed = shortened(1, chunk) * shortened(2, chunk)
        direct[chunk] = mixed
        scatter_rows(chunk, mixed.T, mix_out)
    for half in range(halves):
        send_all(mix_out, mix_in, 1, half)

    for chunk in range(chunks):
        lanes = slice(chunk * LANES, (chunk + 1) * LANES)
        query[chunk] = shortened(0, chunk)
        direct[chunk] = direct[chunk] * gain_ref[:, lanes]

    def transform(landing, half):
        def load(block):
            def get():
                value = landing[half, block]
                angle = 2.0 * math.pi * block / (4 * devices)
                return (value * math.cos(angle), value * math.sin(angle))

            return get

        for k, (real, imag) in enumerate(fft([load(b) for b in range(devices)], 1)):
            cos, sin = (twist_cos[k : k + 1, :], twist_sin[k : k + 1, :])
            rows = slice(k * SUB, (k + 1) * SUB)
            spec_a[rows, :LANES] = real * cos - imag * sin
            spec_a[rows, LANES:] = real * sin + imag * cos
        return dot3(spec_a[...], fwd_hi, fwd_lo)

    for half in range(halves):
        wait_all(filt_in, recv_sems, 0, half)
        spec_h[half] = transform(filt_in, half)

    for half in range(halves):
        wait_all(mix_in, recv_sems, 1, half)
        mixed_spec = transform(mix_in, half)
        mixed_re, mixed_im = (mixed_spec[:, :LANES], mixed_spec[:, LANES:])
        filt_re, filt_im = (spec_h[half, :, :LANES], spec_h[half, :, LANES:])
        spec_a[:, :LANES] = mixed_re * filt_re - mixed_im * filt_im
        spec_a[:, LANES:] = mixed_re * filt_im + mixed_im * filt_re
        spec_g[...] = dot3(spec_a[...], inv_hi, inv_lo)

        def load(k):
            def get():
                rows = slice(k * SUB, (k + 1) * SUB)
                real, imag = (spec_g[rows, :LANES], spec_g[rows, LANES:])
                cos, sin = (twist_cos[k : k + 1, :], twist_sin[k : k + 1, :])
                return (real * cos + imag * sin, imag * cos - real * sin)

            return get

        for block, (real, imag) in enumerate(fft([load(k) for k in range(devices)], -1)):
            angle = 2.0 * math.pi * block / (4 * devices)
            conv_out[half, block] = real * math.cos(angle) + imag * math.sin(angle)
        send_all(conv_out, conv_in, 2, half)

    for half in range(halves):
        wait_all(conv_in, recv_sems, 2, half)
    for chunk in range(chunks):
        lanes = slice(chunk * LANES, (chunk + 1) * LANES)
        pieces = [
            conv_in[half, chunk * per_chunk + part]
            for part in range(per_chunk)
            for half in range(halves)
        ]
        conv = jnp.concatenate(pieces, axis=0).T
        out_ref[:, lanes] = (query[chunk] * (conv + direct[chunk])).astype(out_ref.dtype)
    for half in range(halves):
        wait_all(filt_out, send_sems, 0, half)
        wait_all(mix_out, send_sems, 1, half)
        wait_all(conv_out, send_sems, 2, half)


def split_table(table):
    hi = table.astype(jnp.bfloat16)
    lo = (table - hi.astype(np.float64)).astype(jnp.bfloat16)
    return hi, lo


def tables(devices, positions):
    p = np.arange(positions, dtype=np.float64)
    angle = 2.0 * np.pi * ((p[:, None] * p[None, :]) % positions) / positions
    cos, sin = (np.cos(angle), np.sin(angle))
    forward = np.block([[cos, sin], [-sin, cos]])
    backward = np.block([[cos, -sin], [sin, cos]]) / (devices * positions)
    k = np.arange(devices, dtype=np.float64)
    twist = 2.0 * np.pi * (k[:, None] + 0.25) * p[None, :] / (devices * positions)
    return (
        *split_table(forward),
        *split_table(backward),
        np.cos(twist).astype(np.float32),
        np.sin(twist).astype(np.float32),
    )


def owned_channels(consts, groups, shards, projections, short_taps, long_filter, skip_gain):
    _, positions, channels = projections.shape
    devices = groups * shards
    owned = channels // devices
    halves = owned // SUB
    chunks = channels // LANES
    sizes = (groups, shards, positions, channels, short_taps.shape[1])
    f32, bf16 = (jnp.float32, jnp.bfloat16)
    slabs = pltpu.VMEM((halves, devices, SUB, LANES), f32)
    vmem = pl.BlockSpec(memory_space=pltpu.VMEM)
    return pl.pallas_call(
        functools.partial(owner_kernel, sizes),
        out_shape=jax.ShapeDtypeStruct((positions, channels), bf16),
        in_specs=[vmem] * (4 + len(consts)),
        out_specs=vmem,
        scratch_shapes=[
            pltpu.VMEM((3, HALO, channels), bf16),
            pltpu.VMEM((3, chunks, HALO + positions, LANES), f32),
            pltpu.VMEM((chunks, positions, LANES), f32),
            pltpu.VMEM((chunks, positions, LANES), f32),
            slabs,
            slabs,
            slabs,
            slabs,
            slabs,
            slabs,
            pltpu.VMEM((devices * SUB, 2 * LANES), f32),
            pltpu.VMEM((halves, devices * SUB, 2 * LANES), f32),
            pltpu.VMEM((devices * SUB, 2 * LANES), f32),
            pltpu.SemaphoreType.DMA((2,)),
            pltpu.SemaphoreType.DMA((3, halves)),
            pltpu.SemaphoreType.DMA((3, halves)),
        ],
        compiler_params=pltpu.CompilerParams(collective_id=0, has_side_effects=True),
    )(projections, short_taps, long_filter, skip_gain.reshape(1, channels), *consts)


def on_device(groups, shards, projections, short_taps, long_filter, skip_gain):
    _, positions, channels = projections.shape
    devices = groups * shards
    fits = (
        positions == LANES
        and channels % LANES == 0
        and channels % (SUB * devices) == 0
        and LANES % (channels // devices) == 0
        and devices & (devices - 1) == 0
        and short_taps.shape[1] - 1 <= HALO
    )
    if not fits:
        return per_device(projections, short_taps, long_filter, skip_gain)
    consts = tables(devices, positions)
    return owned_channels(consts, groups, shards, projections, short_taps, long_filter, skip_gain)


def solution(mesh):
    placed = (P(None, ("grp", "shard"), None), P(), P(("grp", "shard"), None), P())
    body = functools.partial(on_device, mesh.shape["grp"], mesh.shape["shard"])
    return jax.shard_map(
        body, mesh=mesh, in_specs=placed, out_specs=P(("grp", "shard"), None), check_vma=False
    )
```

```python
import functools
import math

import jax
import jax.numpy as jnp
import numpy as np
from jax import lax
from jax.experimental import pallas as pl
from jax.experimental.pallas import tpu as pltpu
from jax.sharding import PartitionSpec as P

precise = lax.Precision.HIGHEST


def from_behind(block, axis, distance):
    devices = range(lax.axis_size(axis))
    route = [(i - distance, i) for i in devices if i - distance in devices]
    return lax.ppermute(block, axis, route)


def angles_of(first, second, modulus):
    return (first * second % modulus).astype(jnp.float32) * (2.0 * math.pi / modulus)


def per_device(projections, short_taps, long_filter, skip_gain):
    positions = projections.shape[1]
    channels = projections.shape[2]
    taps_count = short_taps.shape[1]
    groups = lax.axis_size("grp")
    shards = lax.axis_size("shard")
    devices = groups * shards
    span_len = 2 * devices
    length = span_len * positions
    slice_len = positions * channels // devices
    device_id = lax.axis_index("grp") * shards + lax.axis_index("shard")
    rim_rows = from_behind(projections[:, positions - (taps_count - 1) :, :], ("grp", "shard"), 1)
    extended = jnp.concatenate([rim_rows, projections], axis=1)
    shortened = short_taps[:, 0, None, :] * extended[
        :, taps_count - 1 : taps_count - 1 + positions, :
    ].astype(jnp.float32)
    for tap_index in range(1, taps_count):
        shortened = shortened + short_taps[:, tap_index, None, :] * extended[
            :, taps_count - 1 - tap_index : taps_count - 1 - tap_index + positions, :
        ].astype(jnp.float32)
    query = shortened[0]
    mixed = shortened[1] * shortened[2]
    mixed_rows = mixed.reshape(groups, shards, slice_len)
    filt_rows = long_filter.reshape(groups, shards, slice_len)
    got_mixed, got_filt = (
        lax.all_to_all(
            lax.all_to_all(mixed_rows, "grp", split_axis=0, concat_axis=0, tiled=True),
            "shard",
            split_axis=1,
            concat_axis=1,
            tiled=True,
        ),
        lax.all_to_all(
            lax.all_to_all(filt_rows, "grp", split_axis=0, concat_axis=0, tiled=True),
            "shard",
            split_axis=1,
            concat_axis=1,
            tiled=True,
        ),
    )
    dev_ids = jnp.arange(devices, dtype=jnp.int32)
    freq_ids = jnp.arange(span_len, dtype=jnp.int32)
    outer = angles_of(freq_ids[:, None], dev_ids[None, :], span_len)
    outer_cos, outer_sin = (jnp.cos(outer), jnp.sin(outer))
    flat_ids = device_id * slice_len + jnp.arange(slice_len, dtype=jnp.int32)
    row_of = flat_ids // channels
    twist = angles_of(freq_ids[:, None], row_of[None, :], length)
    twist_cos, twist_sin = (jnp.cos(twist), jnp.sin(twist))

    def forward_outer(values):
        flat_values = values.reshape(devices, slice_len)
        real = jnp.dot(outer_cos, flat_values, precision=precise)
        imag = -jnp.dot(outer_sin, flat_values, precision=precise)
        turned_re = real * twist_cos + imag * twist_sin
        turned_im = imag * twist_cos - real * twist_sin
        return (
            turned_re.reshape(2, groups, shards, slice_len),
            turned_im.reshape(2, groups, shards, slice_len),
        )

    mixed_re, mixed_im = forward_outer(got_mixed)
    filt_re, filt_im = forward_outer(got_filt)
    mixed_re, mixed_im, filt_re, filt_im = (
        lax.all_to_all(
            lax.all_to_all(mixed_re, "grp", split_axis=1, concat_axis=1, tiled=True),
            "shard",
            split_axis=2,
            concat_axis=2,
            tiled=True,
        ),
        lax.all_to_all(
            lax.all_to_all(mixed_im, "grp", split_axis=1, concat_axis=1, tiled=True),
            "shard",
            split_axis=2,
            concat_axis=2,
            tiled=True,
        ),
        lax.all_to_all(
            lax.all_to_all(filt_re, "grp", split_axis=1, concat_axis=1, tiled=True),
            "shard",
            split_axis=2,
            concat_axis=2,
            tiled=True,
        ),
        lax.all_to_all(
            lax.all_to_all(filt_im, "grp", split_axis=1, concat_axis=1, tiled=True),
            "shard",
            split_axis=2,
            concat_axis=2,
            tiled=True,
        ),
    )
    row_ids = jnp.arange(positions, dtype=jnp.int32)
    inner = angles_of(row_ids[:, None], row_ids[None, :], positions)
    inner_cos, inner_sin = (jnp.cos(inner), jnp.sin(inner))

    def forward_inner(real, imag):
        real = real.reshape(2, positions, channels)
        imag = imag.reshape(2, positions, channels)
        out_re = jnp.einsum("kp,rpc->rkc", inner_cos, real, precision=precise) + jnp.einsum(
            "kp,rpc->rkc", inner_sin, imag, precision=precise
        )
        out_im = jnp.einsum("kp,rpc->rkc", inner_cos, imag, precision=precise) - jnp.einsum(
            "kp,rpc->rkc", inner_sin, real, precision=precise
        )
        return (out_re, out_im)

    spec_mixed_re, spec_mixed_im = forward_inner(mixed_re, mixed_im)
    spec_filt_re, spec_filt_im = forward_inner(filt_re, filt_im)
    prod_re = spec_mixed_re * spec_filt_re - spec_mixed_im * spec_filt_im
    prod_im = spec_mixed_re * spec_filt_im + spec_mixed_im * spec_filt_re
    back_re = jnp.einsum("kp,rkc->rpc", inner_cos, prod_re, precision=precise) - jnp.einsum(
        "kp,rkc->rpc", inner_sin, prod_im, precision=precise
    )
    back_im = jnp.einsum("kp,rkc->rpc", inner_cos, prod_im, precision=precise) + jnp.einsum(
        "kp,rkc->rpc", inner_sin, prod_re, precision=precise
    )
    own_freqs = jnp.arange(2, dtype=jnp.int32) * devices + device_id
    back_twist = angles_of(own_freqs[:, None], row_ids[None, :], length)
    back_cos, back_sin = (jnp.cos(back_twist)[:, :, None], jnp.sin(back_twist)[:, :, None])
    rot_re = (back_re * back_cos - back_im * back_sin).reshape(2, groups, shards, slice_len)
    rot_im = (back_re * back_sin + back_im * back_cos).reshape(2, groups, shards, slice_len)
    rot_re, rot_im = (
        lax.all_to_all(
            lax.all_to_all(rot_re, "grp", split_axis=1, concat_axis=1, tiled=True),
            "shard",
            split_axis=2,
            concat_axis=2,
            tiled=True,
        ),
        lax.all_to_all(
            lax.all_to_all(rot_im, "grp", split_axis=1, concat_axis=1, tiled=True),
            "shard",
            split_axis=2,
            concat_axis=2,
            tiled=True,
        ),
    )
    rot_re = rot_re.reshape(span_len, slice_len)
    rot_im = rot_im.reshape(span_len, slice_len)
    values = (
        jnp.einsum("kd,kf->df", outer_cos, rot_re, precision=precise)
        - jnp.einsum("kd,kf->df", outer_sin, rot_im, precision=precise)
    ) / length
    values = values.reshape(groups, shards, slice_len)
    conv_rows = lax.all_to_all(
        lax.all_to_all(values, "grp", split_axis=0, concat_axis=0, tiled=True),
        "shard",
        split_axis=1,
        concat_axis=1,
        tiled=True,
    )
    conv = conv_rows.reshape(positions, channels)
    return (query * (conv + skip_gain * mixed)).astype(jnp.bfloat16)


MESH = pl.DeviceIdType.MESH
LANES = 128
SUB = 8
HALO = 16
TOGETHER = 4


def turned(value, numerator, denominator):
    numerator %= denominator
    real, imag = value
    eighths, rest = divmod(8 * numerator, denominator)
    if rest == 0:
        half = math.sqrt(0.5)
        if eighths == 0:
            return (real, imag)
        if eighths == 2:
            return (-imag, real)
        if eighths == 4:
            return (-real, -imag)
        if eighths == 6:
            return (imag, -real)
        if eighths == 1:
            return ((real - imag) * half, (real + imag) * half)
        if eighths == 3:
            return ((real + imag) * -half, (real - imag) * half)
        if eighths == 5:
            return ((imag - real) * half, (real + imag) * -half)
        return ((real + imag) * half, (imag - real) * half)
    angle = 2.0 * math.pi * numerator / denominator
    cos, sin = (math.cos(angle), math.sin(angle))
    return (real * cos - imag * sin, real * sin + imag * cos)


def fft(loads, sign):
    count = len(loads)
    if count == 1:
        return [loads[0]()]
    even, odd = (fft(loads[::2], sign), fft(loads[1::2], sign))
    low, high = ([], [])
    for k in range(count // 2):
        moved = turned(odd[k], sign * k, count)
        low.append((even[k][0] + moved[0], even[k][1] + moved[1]))
        high.append((even[k][0] - moved[0], even[k][1] - moved[1]))
    return low + high


def dot3(values, table_hi, table_lo):
    hi = values.astype(jnp.bfloat16)
    lo = (values - hi.astype(jnp.float32)).astype(jnp.bfloat16)
    dot = functools.partial(jnp.dot, preferred_element_type=jnp.float32)
    return dot(hi, table_hi[...]) + (dot(lo, table_hi[...]) + dot(hi, table_lo[...]))


def owner_kernel(
    sizes,
    proj_ref,
    taps_ref,
    held_ref,
    gain_ref,
    fwd_hi,
    fwd_lo,
    inv_hi,
    inv_lo,
    twist_cos,
    twist_sin,
    out_ref,
    rim,
    ext,
    query,
    direct,
    filt_out,
    pair_out,
    filt_in,
    pair_in,
    mix_in,
    tap_rows,
    tap_columns,
    conv_out,
    conv_in,
    spec_a,
    spec_held,
    spec_g,
    rim_sems,
    send_sems,
    recv_sems,
):
    groups, shards, positions, channels, taps = sizes
    devices = groups * shards
    owned = channels // devices
    halves = owned // SUB
    per_chunk = LANES // owned
    chunks = channels // LANES
    my_group, my_shard = (lax.axis_index("grp"), lax.axis_index("shard"))
    me = my_group * shards + my_shard

    def partners(act):
        for apart in range(devices - 1, 0, -1):
            group = jnp.bitwise_xor(my_group, apart // shards)
            shard = jnp.bitwise_xor(my_shard, apart % shards)
            act((group, shard), group * shards + shard)

    def place(target):
        return (target // shards, target % shards)

    barrier = pltpu.get_barrier_semaphore()
    partners(
        lambda there, target: pl.semaphore_signal(
            barrier, inc=1, device_id=there, device_id_type=MESH
        )
    )

    def scatter_rows(chunk, turned_block, store):
        for part in range(per_chunk):
            for half in range(halves):
                first = part * owned + half * SUB
                store[half, chunk * per_chunk + part] = turned_block[first : first + SUB, :]

    for chunk in range(chunks):
        lanes = slice(chunk * LANES, (chunk + 1) * LANES)
        scatter_rows(chunk, held_ref[:, lanes].T, filt_out)
        for which in range(3):
            ext[which, chunk, HALO:, :] = proj_ref[which, :, lanes].astype(jnp.float32)
        tap_rows[...] = jnp.zeros_like(tap_rows)
        for pair in range(2):
            block = ext[pair + 1, chunk, HALO:, :].T.astype(jnp.bfloat16)
            for part in range(per_chunk):
                rows = slice(part * owned, (part + 1) * owned)
                pair_out[pair, chunk * per_chunk + part] = block[rows, :]
            tap_rows[pair * HALO : pair * HALO + taps, :] = taps_ref[pair + 1, :, lanes]
        block = tap_rows[...].T
        for part in range(per_chunk):
            tap_columns[chunk * per_chunk + part] = block[part * owned : (part + 1) * owned, :]
    for pair in range(2):
        pair_in[pair, 0] = jnp.zeros((owned, LANES), jnp.bfloat16)

    pl.semaphore_wait(barrier, devices - 1)

    rim_copy = pltpu.make_async_remote_copy(
        src_ref=proj_ref.at[:, positions - HALO :, :],
        dst_ref=rim,
        send_sem=rim_sems.at[0],
        recv_sem=rim_sems.at[1],
        device_id=place(lax.rem(me + 1, devices)),
        device_id_type=MESH,
    )

    def send_all(source, landing, kind, half, shift=0):
        def send(there, target):
            pltpu.make_async_remote_copy(
                src_ref=source.at[half, target],
                dst_ref=landing.at[half, me + shift],
                send_sem=send_sems.at[kind, half],
                recv_sem=recv_sems.at[kind, half],
                device_id=there,
                device_id_type=MESH,
            ).start()

        partners(send)
        landing[half, me + shift] = source[half, me]

    def wait_all(landing, sems, kind, half):
        others = landing.at[half, pl.ds(0, devices - 1)]
        pltpu.make_async_copy(others, others, sems.at[kind, half]).wait()

    for pair in range(2):
        send_all(pair_out, pair_in, 0, pair, 1)
    for half in range(halves):
        send_all(filt_out, filt_in, 1, half)

    rim_copy.start()

    def transform(landing, half):
        def load(block):
            def get():
                value = landing[half, block]
                angle = 2.0 * math.pi * block / (4 * devices)
                return (value * math.cos(angle), value * math.sin(angle))

            return get

        for k, (real, imag) in enumerate(fft([load(b) for b in range(devices)], 1)):
            cos, sin = (twist_cos[k : k + 1, :], twist_sin[k : k + 1, :])
            rows = slice(k * SUB, (k + 1) * SUB)
            spec_a[rows, :LANES] = real * cos - imag * sin
            spec_a[rows, LANES:] = real * sin + imag * cos
        return dot3(spec_a[...], fwd_hi, fwd_lo)

    for pair in range(2):
        wait_all(pair_in, recv_sems, 0, pair)
    own_taps = tap_columns[me]

    @pl.loop(0, devices // TOGETHER)
    def _(step):
        lane = lax.broadcasted_iota(jnp.int32, (TOGETHER, owned, LANES), 2)

        def convolved(pair):
            before = pair_in[pair, pl.ds(step * TOGETHER, TOGETHER)].astype(jnp.float32)
            block = pair_in[pair, pl.ds(step * TOGETHER + 1, TOGETHER)].astype(jnp.float32)
            total = None
            for tap in range(taps):
                moved = block
                if tap:
                    moved = pltpu.roll(jnp.where(lane >= LANES - tap, before, block), tap, 2)
                column = pair * HALO + tap
                term = own_taps[:, column : column + 1][None] * moved
                total = term if total is None else total + term
            return total

        mixed = convolved(0) * convolved(1)
        for half in range(halves):
            rows = slice(half * SUB, (half + 1) * SUB)
            mix_in[half, pl.ds(step * TOGETHER, TOGETHER)] = mixed[:, rows, :]

    for half in range(halves):
        spec_held[half] = transform(mix_in, half)

    for half in range(halves):
        wait_all(filt_in, recv_sems, 1, half)
        far_spec = transform(filt_in, half)
        far_re, far_im = (far_spec[:, :LANES], far_spec[:, LANES:])
        held_re, held_im = (spec_held[half, :, :LANES], spec_held[half, :, LANES:])
        spec_a[:, :LANES] = far_re * held_re - far_im * held_im
        spec_a[:, LANES:] = far_re * held_im + far_im * held_re
        spec_g[...] = dot3(spec_a[...], inv_hi, inv_lo)

        def load(k):
            def get():
                rows = slice(k * SUB, (k + 1) * SUB)
                real, imag = (spec_g[rows, :LANES], spec_g[rows, LANES:])
                cos, sin = (twist_cos[k : k + 1, :], twist_sin[k : k + 1, :])
                return (real * cos + imag * sin, imag * cos - real * sin)

            return get

        for block, (real, imag) in enumerate(fft([load(k) for k in range(devices)], -1)):
            angle = 2.0 * math.pi * block / (4 * devices)
            conv_out[half, block] = real * math.cos(angle) + imag * math.sin(angle)
        send_all(conv_out, conv_in, 2, half)

    rim_copy.wait()
    keep = jnp.where(me > 0, 1.0, 0.0).astype(jnp.float32)
    for chunk in range(chunks):
        lanes = slice(chunk * LANES, (chunk + 1) * LANES)
        for which in range(3):
            ext[which, chunk, :HALO, :] = rim[which, :, lanes].astype(jnp.float32) * keep

    def shortened(which, chunk):
        lanes = slice(chunk * LANES, (chunk + 1) * LANES)
        total = None
        for tap in range(taps):
            term = taps_ref[which, tap : tap + 1, lanes] * ext[
                which, chunk, HALO - tap : HALO - tap + positions, :
            ]
            total = term if total is None else total + term
        return total

    for chunk in range(chunks):
        lanes = slice(chunk * LANES, (chunk + 1) * LANES)
        query[chunk] = shortened(0, chunk)
        direct[chunk] = shortened(1, chunk) * shortened(2, chunk) * gain_ref[:, lanes]

    for half in range(halves):
        wait_all(conv_in, recv_sems, 2, half)
    for chunk in range(chunks):
        lanes = slice(chunk * LANES, (chunk + 1) * LANES)
        pieces = [
            conv_in[half, chunk * per_chunk + part]
            for part in range(per_chunk)
            for half in range(halves)
        ]
        conv = jnp.concatenate(pieces, axis=0).T
        out_ref[:, lanes] = (query[chunk] * (conv + direct[chunk])).astype(out_ref.dtype)
    for pair in range(2):
        wait_all(pair_in, send_sems, 0, pair)
    for half in range(halves):
        wait_all(filt_out, send_sems, 1, half)
        wait_all(conv_out, send_sems, 2, half)


def split_table(table):
    hi = table.astype(jnp.bfloat16)
    lo = (table - hi.astype(np.float64)).astype(jnp.bfloat16)
    return hi, lo


def tables(devices, positions):
    p = np.arange(positions, dtype=np.float64)
    angle = 2.0 * np.pi * ((p[:, None] * p[None, :]) % positions) / positions
    cos, sin = (np.cos(angle), np.sin(angle))
    forward = np.block([[cos, sin], [-sin, cos]])
    backward = np.block([[cos, -sin], [sin, cos]]) / (devices * positions)
    k = np.arange(devices, dtype=np.float64)
    twist = 2.0 * np.pi * (k[:, None] + 0.25) * p[None, :] / (devices * positions)
    return (
        *split_table(forward),
        *split_table(backward),
        np.cos(twist).astype(np.float32),
        np.sin(twist).astype(np.float32),
    )


def owned_channels(consts, groups, shards, projections, short_taps, long_filter, skip_gain):
    _, positions, channels = projections.shape
    devices = groups * shards
    owned = channels // devices
    halves = owned // SUB
    chunks = channels // LANES
    sizes = (groups, shards, positions, channels, short_taps.shape[1])
    f32, bf16 = (jnp.float32, jnp.bfloat16)
    slabs = pltpu.VMEM((halves, devices, SUB, LANES), f32)
    vmem = pl.BlockSpec(memory_space=pltpu.VMEM)
    return pl.pallas_call(
        functools.partial(owner_kernel, sizes),
        out_shape=jax.ShapeDtypeStruct((positions, channels), bf16),
        in_specs=[vmem] * (4 + len(consts)),
        out_specs=vmem,
        scratch_shapes=[
            pltpu.VMEM((3, HALO, channels), bf16),
            pltpu.VMEM((3, chunks, HALO + positions, LANES), f32),
            pltpu.VMEM((chunks, positions, LANES), f32),
            pltpu.VMEM((chunks, positions, LANES), f32),
            slabs,
            pltpu.VMEM((2, devices, owned, LANES), bf16),
            slabs,
            pltpu.VMEM((2, devices + 1, owned, LANES), bf16),
            slabs,
            pltpu.VMEM((LANES, LANES), f32),
            pltpu.VMEM((devices, owned, LANES), f32),
            slabs,
            slabs,
            pltpu.VMEM((devices * SUB, 2 * LANES), f32),
            pltpu.VMEM((halves, devices * SUB, 2 * LANES), f32),
            pltpu.VMEM((devices * SUB, 2 * LANES), f32),
            pltpu.SemaphoreType.DMA((2,)),
            pltpu.SemaphoreType.DMA((3, max(halves, 2))),
            pltpu.SemaphoreType.DMA((3, max(halves, 2))),
        ],
        compiler_params=pltpu.CompilerParams(collective_id=0, has_side_effects=True),
    )(projections, short_taps, long_filter, skip_gain.reshape(1, channels), *consts)


def on_device(groups, shards, projections, short_taps, long_filter, skip_gain):
    _, positions, channels = projections.shape
    devices = groups * shards
    fits = (
        positions == LANES
        and channels % LANES == 0
        and channels % (SUB * devices) == 0
        and LANES % (channels // devices) == 0
        and devices & (devices - 1) == 0
        and (channels // devices) % 16 == 0
        and devices % TOGETHER == 0
        and short_taps.shape[1] <= HALO
    )
    if not fits:
        return per_device(projections, short_taps, long_filter, skip_gain)
    consts = tables(devices, positions)
    return owned_channels(consts, groups, shards, projections, short_taps, long_filter, skip_gain)


def solution(mesh):
    placed = (P(None, ("grp", "shard"), None), P(), P(("grp", "shard"), None), P())
    body = functools.partial(on_device, mesh.shape["grp"], mesh.shape["shard"])
    return jax.shard_map(
        body, mesh=mesh, in_specs=placed, out_specs=P(("grp", "shard"), None), check_vma=False
    )
```

```python
import functools
import math

import jax
import jax.numpy as jnp
import numpy as np
from jax import lax
from jax.experimental import pallas as pl
from jax.experimental.pallas import tpu as pltpu
from jax.sharding import PartitionSpec as P

precise = lax.Precision.HIGHEST


def from_behind(block, axis, distance):
    devices = range(lax.axis_size(axis))
    route = [(i - distance, i) for i in devices if i - distance in devices]
    return lax.ppermute(block, axis, route)


def angles_of(first, second, modulus):
    return (first * second % modulus).astype(jnp.float32) * (2.0 * math.pi / modulus)


def per_device(projections, short_taps, long_filter, skip_gain):
    positions = projections.shape[1]
    channels = projections.shape[2]
    taps_count = short_taps.shape[1]
    groups = lax.axis_size("grp")
    shards = lax.axis_size("shard")
    devices = groups * shards
    span_len = 2 * devices
    length = span_len * positions
    slice_len = positions * channels // devices
    device_id = lax.axis_index("grp") * shards + lax.axis_index("shard")
    rim_rows = from_behind(projections[:, positions - (taps_count - 1) :, :], ("grp", "shard"), 1)
    extended = jnp.concatenate([rim_rows, projections], axis=1)
    shortened = short_taps[:, 0, None, :] * extended[
        :, taps_count - 1 : taps_count - 1 + positions, :
    ].astype(jnp.float32)
    for tap_index in range(1, taps_count):
        shortened = shortened + short_taps[:, tap_index, None, :] * extended[
            :, taps_count - 1 - tap_index : taps_count - 1 - tap_index + positions, :
        ].astype(jnp.float32)
    query = shortened[0]
    mixed = shortened[1] * shortened[2]
    mixed_rows = mixed.reshape(groups, shards, slice_len)
    filt_rows = long_filter.reshape(groups, shards, slice_len)
    got_mixed, got_filt = (
        lax.all_to_all(
            lax.all_to_all(mixed_rows, "grp", split_axis=0, concat_axis=0, tiled=True),
            "shard",
            split_axis=1,
            concat_axis=1,
            tiled=True,
        ),
        lax.all_to_all(
            lax.all_to_all(filt_rows, "grp", split_axis=0, concat_axis=0, tiled=True),
            "shard",
            split_axis=1,
            concat_axis=1,
            tiled=True,
        ),
    )
    dev_ids = jnp.arange(devices, dtype=jnp.int32)
    freq_ids = jnp.arange(span_len, dtype=jnp.int32)
    outer = angles_of(freq_ids[:, None], dev_ids[None, :], span_len)
    outer_cos, outer_sin = (jnp.cos(outer), jnp.sin(outer))
    flat_ids = device_id * slice_len + jnp.arange(slice_len, dtype=jnp.int32)
    row_of = flat_ids // channels
    twist = angles_of(freq_ids[:, None], row_of[None, :], length)
    twist_cos, twist_sin = (jnp.cos(twist), jnp.sin(twist))

    def forward_outer(values):
        flat_values = values.reshape(devices, slice_len)
        real = jnp.dot(outer_cos, flat_values, precision=precise)
        imag = -jnp.dot(outer_sin, flat_values, precision=precise)
        turned_re = real * twist_cos + imag * twist_sin
        turned_im = imag * twist_cos - real * twist_sin
        return (
            turned_re.reshape(2, groups, shards, slice_len),
            turned_im.reshape(2, groups, shards, slice_len),
        )

    mixed_re, mixed_im = forward_outer(got_mixed)
    filt_re, filt_im = forward_outer(got_filt)
    mixed_re, mixed_im, filt_re, filt_im = (
        lax.all_to_all(
            lax.all_to_all(mixed_re, "grp", split_axis=1, concat_axis=1, tiled=True),
            "shard",
            split_axis=2,
            concat_axis=2,
            tiled=True,
        ),
        lax.all_to_all(
            lax.all_to_all(mixed_im, "grp", split_axis=1, concat_axis=1, tiled=True),
            "shard",
            split_axis=2,
            concat_axis=2,
            tiled=True,
        ),
        lax.all_to_all(
            lax.all_to_all(filt_re, "grp", split_axis=1, concat_axis=1, tiled=True),
            "shard",
            split_axis=2,
            concat_axis=2,
            tiled=True,
        ),
        lax.all_to_all(
            lax.all_to_all(filt_im, "grp", split_axis=1, concat_axis=1, tiled=True),
            "shard",
            split_axis=2,
            concat_axis=2,
            tiled=True,
        ),
    )
    row_ids = jnp.arange(positions, dtype=jnp.int32)
    inner = angles_of(row_ids[:, None], row_ids[None, :], positions)
    inner_cos, inner_sin = (jnp.cos(inner), jnp.sin(inner))

    def forward_inner(real, imag):
        real = real.reshape(2, positions, channels)
        imag = imag.reshape(2, positions, channels)
        out_re = jnp.einsum("kp,rpc->rkc", inner_cos, real, precision=precise) + jnp.einsum(
            "kp,rpc->rkc", inner_sin, imag, precision=precise
        )
        out_im = jnp.einsum("kp,rpc->rkc", inner_cos, imag, precision=precise) - jnp.einsum(
            "kp,rpc->rkc", inner_sin, real, precision=precise
        )
        return (out_re, out_im)

    spec_mixed_re, spec_mixed_im = forward_inner(mixed_re, mixed_im)
    spec_filt_re, spec_filt_im = forward_inner(filt_re, filt_im)
    prod_re = spec_mixed_re * spec_filt_re - spec_mixed_im * spec_filt_im
    prod_im = spec_mixed_re * spec_filt_im + spec_mixed_im * spec_filt_re
    back_re = jnp.einsum("kp,rkc->rpc", inner_cos, prod_re, precision=precise) - jnp.einsum(
        "kp,rkc->rpc", inner_sin, prod_im, precision=precise
    )
    back_im = jnp.einsum("kp,rkc->rpc", inner_cos, prod_im, precision=precise) + jnp.einsum(
        "kp,rkc->rpc", inner_sin, prod_re, precision=precise
    )
    own_freqs = jnp.arange(2, dtype=jnp.int32) * devices + device_id
    back_twist = angles_of(own_freqs[:, None], row_ids[None, :], length)
    back_cos, back_sin = (jnp.cos(back_twist)[:, :, None], jnp.sin(back_twist)[:, :, None])
    rot_re = (back_re * back_cos - back_im * back_sin).reshape(2, groups, shards, slice_len)
    rot_im = (back_re * back_sin + back_im * back_cos).reshape(2, groups, shards, slice_len)
    rot_re, rot_im = (
        lax.all_to_all(
            lax.all_to_all(rot_re, "grp", split_axis=1, concat_axis=1, tiled=True),
            "shard",
            split_axis=2,
            concat_axis=2,
            tiled=True,
        ),
        lax.all_to_all(
            lax.all_to_all(rot_im, "grp", split_axis=1, concat_axis=1, tiled=True),
            "shard",
            split_axis=2,
            concat_axis=2,
            tiled=True,
        ),
    )
    rot_re = rot_re.reshape(span_len, slice_len)
    rot_im = rot_im.reshape(span_len, slice_len)
    values = (
        jnp.einsum("kd,kf->df", outer_cos, rot_re, precision=precise)
        - jnp.einsum("kd,kf->df", outer_sin, rot_im, precision=precise)
    ) / length
    values = values.reshape(groups, shards, slice_len)
    conv_rows = lax.all_to_all(
        lax.all_to_all(values, "grp", split_axis=0, concat_axis=0, tiled=True),
        "shard",
        split_axis=1,
        concat_axis=1,
        tiled=True,
    )
    conv = conv_rows.reshape(positions, channels)
    return (query * (conv + skip_gain * mixed)).astype(jnp.bfloat16)


MESH = pl.DeviceIdType.MESH
LANES = 128
SUB = 8
HALO = 16
TOGETHER = 4


def turned(value, numerator, denominator):
    numerator %= denominator
    real, imag = value
    eighths, rest = divmod(8 * numerator, denominator)
    if rest == 0:
        half = math.sqrt(0.5)
        if eighths == 0:
            return (real, imag)
        if eighths == 2:
            return (-imag, real)
        if eighths == 4:
            return (-real, -imag)
        if eighths == 6:
            return (imag, -real)
        if eighths == 1:
            return ((real - imag) * half, (real + imag) * half)
        if eighths == 3:
            return ((real + imag) * -half, (real - imag) * half)
        if eighths == 5:
            return ((imag - real) * half, (real + imag) * -half)
        return ((real + imag) * half, (imag - real) * half)
    angle = 2.0 * math.pi * numerator / denominator
    cos, sin = (math.cos(angle), math.sin(angle))
    return (real * cos - imag * sin, real * sin + imag * cos)


def fft(loads, sign):
    count = len(loads)
    if count == 1:
        return [loads[0]()]
    even, odd = (fft(loads[::2], sign), fft(loads[1::2], sign))
    low, high = ([], [])
    for k in range(count // 2):
        moved = turned(odd[k], sign * k, count)
        low.append((even[k][0] + moved[0], even[k][1] + moved[1]))
        high.append((even[k][0] - moved[0], even[k][1] - moved[1]))
    return low + high


def dot3(values, table_hi, table_lo):
    hi = values.astype(jnp.bfloat16)
    lo = (values - hi.astype(jnp.float32)).astype(jnp.bfloat16)
    dot = functools.partial(jnp.dot, preferred_element_type=jnp.float32)
    return dot(hi, table_hi[...]) + (dot(lo, table_hi[...]) + dot(hi, table_lo[...]))


def owner_kernel(
    sizes,
    proj_ref_far,
    taps_ref_far,
    filt_ref_far,
    gain_ref_far,
    fwd_hi_far,
    fwd_lo_far,
    inv_hi_far,
    inv_lo_far,
    twist_cos_far,
    twist_sin_far,
    out_ref,
    proj_ref,
    taps_ref,
    filt_ref,
    gain_ref,
    fwd_hi,
    fwd_lo,
    inv_hi,
    inv_lo,
    twist_cos,
    twist_sin,
    rim,
    ext,
    query,
    direct,
    filt_out,
    pair_out,
    filt_in,
    pair_in,
    mix_in,
    tap_rows,
    tap_columns,
    conv_out,
    conv_in,
    spec_a,
    spec_held,
    spec_g,
    load_sems,
    rim_sems,
    send_sems,
    recv_sems,
):
    groups, shards, positions, channels, taps = sizes
    devices = groups * shards
    owned = channels // devices
    halves = owned // SUB
    per_chunk = LANES // owned
    chunks = channels // LANES
    my_group, my_shard = (lax.axis_index("grp"), lax.axis_index("shard"))
    me = my_group * shards + my_shard

    def partners(act):
        for apart in range(devices - 1, 0, -1):
            group = jnp.bitwise_xor(my_group, apart // shards)
            shard = jnp.bitwise_xor(my_shard, apart % shards)
            act((group, shard), group * shards + shard)

    def place(target):
        return (target // shards, target % shards)

    barrier = pltpu.get_barrier_semaphore()
    partners(
        lambda there, target: pl.semaphore_signal(
            barrier, inc=1, device_id=there, device_id_type=MESH
        )
    )

    def scatter_rows(chunk, turned_block, store):
        for part in range(per_chunk):
            for half in range(halves):
                first = part * owned + half * SUB
                store[half, chunk * per_chunk + part] = turned_block[first : first + SUB, :]

    far = (proj_ref_far, filt_ref_far, taps_ref_far, gain_ref_far, fwd_hi_far, fwd_lo_far)
    far += (inv_hi_far, inv_lo_far, twist_cos_far, twist_sin_far)
    near = (proj_ref, filt_ref, taps_ref, gain_ref, fwd_hi, fwd_lo)
    near += (inv_hi, inv_lo, twist_cos, twist_sin)
    loads = [
        pltpu.make_async_copy(source_ref, here_ref, load_sems.at[which])
        for which, (source_ref, here_ref) in enumerate(zip(far, near))
    ]
    for load in loads:
        load.start()
    for load in loads[:3]:
        load.wait()

    for chunk in range(chunks):
        lanes = slice(chunk * LANES, (chunk + 1) * LANES)
        scatter_rows(chunk, filt_ref[:, lanes].T, filt_out)
        for which in range(3):
            ext[which, chunk, HALO:, :] = proj_ref[which, :, lanes].astype(jnp.float32)
        tap_rows[...] = jnp.zeros_like(tap_rows)
        for pair in range(2):
            block = ext[pair + 1, chunk, HALO:, :].T.astype(jnp.bfloat16)
            for part in range(per_chunk):
                rows = slice(part * owned, (part + 1) * owned)
                pair_out[pair, chunk * per_chunk + part] = block[rows, :]
            tap_rows[pair * HALO : pair * HALO + taps, :] = taps_ref[pair + 1, :, lanes]
        block = tap_rows[...].T
        for part in range(per_chunk):
            tap_columns[chunk * per_chunk + part] = block[part * owned : (part + 1) * owned, :]
    for pair in range(2):
        pair_in[pair, 0] = jnp.zeros((owned, LANES), jnp.bfloat16)

    for load in loads[3:]:
        load.wait()
    pl.semaphore_wait(barrier, devices - 1)

    rim_copy = pltpu.make_async_remote_copy(
        src_ref=proj_ref.at[:, positions - HALO :, :],
        dst_ref=rim,
        send_sem=rim_sems.at[0],
        recv_sem=rim_sems.at[1],
        device_id=place(lax.rem(me + 1, devices)),
        device_id_type=MESH,
    )

    def send_all(source, landing, kind, half, shift=0):
        def send(there, target):
            pltpu.make_async_remote_copy(
                src_ref=source.at[half, target],
                dst_ref=landing.at[half, me + shift],
                send_sem=send_sems.at[kind, half],
                recv_sem=recv_sems.at[kind, half],
                device_id=there,
                device_id_type=MESH,
            ).start()

        partners(send)
        landing[half, me + shift] = source[half, me]

    def wait_all(landing, sems, kind, half):
        others = landing.at[half, pl.ds(0, devices - 1)]
        pltpu.make_async_copy(others, others, sems.at[kind, half]).wait()

    for pair in range(2):
        send_all(pair_out, pair_in, 0, pair, 1)
    for half in range(halves):
        send_all(filt_out, filt_in, 1, half)

    rim_copy.start()

    def transform(landing, half):
        def load(block):
            def get():
                value = landing[half, block]
                angle = 2.0 * math.pi * block / (4 * devices)
                return (value * math.cos(angle), value * math.sin(angle))

            return get

        for k, (real, imag) in enumerate(fft([load(b) for b in range(devices)], 1)):
            cos, sin = (twist_cos[k : k + 1, :], twist_sin[k : k + 1, :])
            rows = slice(k * SUB, (k + 1) * SUB)
            spec_a[rows, :LANES] = real * cos - imag * sin
            spec_a[rows, LANES:] = real * sin + imag * cos
        return dot3(spec_a[...], fwd_hi, fwd_lo)

    for pair in range(2):
        wait_all(pair_in, recv_sems, 0, pair)
    own_taps = tap_columns[me]

    @pl.loop(0, devices // TOGETHER)
    def _(step):
        lane = lax.broadcasted_iota(jnp.int32, (TOGETHER, owned, LANES), 2)

        def convolved(pair):
            before = pair_in[pair, pl.ds(step * TOGETHER, TOGETHER)].astype(jnp.float32)
            block = pair_in[pair, pl.ds(step * TOGETHER + 1, TOGETHER)].astype(jnp.float32)
            total = None
            for tap in range(taps):
                moved = block
                if tap:
                    moved = pltpu.roll(jnp.where(lane >= LANES - tap, before, block), tap, 2)
                column = pair * HALO + tap
                term = own_taps[:, column : column + 1][None] * moved
                total = term if total is None else total + term
            return total

        mixed = convolved(0) * convolved(1)
        for half in range(halves):
            rows = slice(half * SUB, (half + 1) * SUB)
            mix_in[half, pl.ds(step * TOGETHER, TOGETHER)] = mixed[:, rows, :]

    for half in range(halves):
        spec_held[half] = transform(mix_in, half)

    for half in range(halves):
        wait_all(filt_in, recv_sems, 1, half)
        far_spec = transform(filt_in, half)
        far_re, far_im = (far_spec[:, :LANES], far_spec[:, LANES:])
        held_re, held_im = (spec_held[half, :, :LANES], spec_held[half, :, LANES:])
        spec_a[:, :LANES] = far_re * held_re - far_im * held_im
        spec_a[:, LANES:] = far_re * held_im + far_im * held_re
        spec_g[...] = dot3(spec_a[...], inv_hi, inv_lo)

        def load(k):
            def get():
                rows = slice(k * SUB, (k + 1) * SUB)
                real, imag = (spec_g[rows, :LANES], spec_g[rows, LANES:])
                cos, sin = (twist_cos[k : k + 1, :], twist_sin[k : k + 1, :])
                return (real * cos + imag * sin, imag * cos - real * sin)

            return get

        for block, (real, imag) in enumerate(fft([load(k) for k in range(devices)], -1)):
            angle = 2.0 * math.pi * block / (4 * devices)
            conv_out[half, block] = real * math.cos(angle) + imag * math.sin(angle)
        send_all(conv_out, conv_in, 2, half)

    rim_copy.wait()
    keep = jnp.where(me > 0, 1.0, 0.0).astype(jnp.float32)
    for chunk in range(chunks):
        lanes = slice(chunk * LANES, (chunk + 1) * LANES)
        for which in range(3):
            ext[which, chunk, :HALO, :] = rim[which, :, lanes].astype(jnp.float32) * keep

    def shortened(which, chunk):
        lanes = slice(chunk * LANES, (chunk + 1) * LANES)
        total = None
        for tap in range(taps):
            term = taps_ref[which, tap : tap + 1, lanes] * ext[
                which, chunk, HALO - tap : HALO - tap + positions, :
            ]
            total = term if total is None else total + term
        return total

    for chunk in range(chunks):
        lanes = slice(chunk * LANES, (chunk + 1) * LANES)
        query[chunk] = shortened(0, chunk)
        direct[chunk] = shortened(1, chunk) * shortened(2, chunk) * gain_ref[:, lanes]

    for half in range(halves):
        wait_all(conv_in, recv_sems, 2, half)
    for chunk in range(chunks):
        lanes = slice(chunk * LANES, (chunk + 1) * LANES)
        pieces = [
            conv_in[half, chunk * per_chunk + part]
            for part in range(per_chunk)
            for half in range(halves)
        ]
        conv = jnp.concatenate(pieces, axis=0).T
        out_ref[:, lanes] = (query[chunk] * (conv + direct[chunk])).astype(out_ref.dtype)
    for pair in range(2):
        wait_all(pair_in, send_sems, 0, pair)
    for half in range(halves):
        wait_all(filt_out, send_sems, 1, half)
        wait_all(conv_out, send_sems, 2, half)


def split_table(table):
    hi = table.astype(jnp.bfloat16)
    lo = (table - hi.astype(np.float64)).astype(jnp.bfloat16)
    return hi, lo


def tables(devices, positions):
    p = np.arange(positions, dtype=np.float64)
    angle = 2.0 * np.pi * ((p[:, None] * p[None, :]) % positions) / positions
    cos, sin = (np.cos(angle), np.sin(angle))
    forward = np.block([[cos, sin], [-sin, cos]])
    backward = np.block([[cos, -sin], [sin, cos]]) / (devices * positions)
    k = np.arange(devices, dtype=np.float64)
    twist = 2.0 * np.pi * (k[:, None] + 0.25) * p[None, :] / (devices * positions)
    return (
        *split_table(forward),
        *split_table(backward),
        np.cos(twist).astype(np.float32),
        np.sin(twist).astype(np.float32),
    )


def owned_channels(consts, groups, shards, projections, short_taps, long_filter, skip_gain):
    _, positions, channels = projections.shape
    devices = groups * shards
    owned = channels // devices
    halves = owned // SUB
    chunks = channels // LANES
    sizes = (groups, shards, positions, channels, short_taps.shape[1])
    f32, bf16 = (jnp.float32, jnp.bfloat16)
    operands = (projections, short_taps, long_filter, skip_gain.reshape(1, channels), *consts)
    slabs = pltpu.VMEM((halves, devices, SUB, LANES), f32)
    vmem = pl.BlockSpec(memory_space=pltpu.VMEM)
    return pl.pallas_call(
        functools.partial(owner_kernel, sizes),
        out_shape=jax.ShapeDtypeStruct((positions, channels), bf16),
        in_specs=[pl.BlockSpec(memory_space=pl.ANY)] * (4 + len(consts)),
        out_specs=vmem,
        scratch_shapes=[
            *(pltpu.VMEM(operand.shape, operand.dtype) for operand in operands),
            pltpu.VMEM((3, HALO, channels), bf16),
            pltpu.VMEM((3, chunks, HALO + positions, LANES), f32),
            pltpu.VMEM((chunks, positions, LANES), f32),
            pltpu.VMEM((chunks, positions, LANES), f32),
            slabs,
            pltpu.VMEM((2, devices, owned, LANES), bf16),
            slabs,
            pltpu.VMEM((2, devices + 1, owned, LANES), bf16),
            slabs,
            pltpu.VMEM((LANES, LANES), f32),
            pltpu.VMEM((devices, owned, LANES), f32),
            slabs,
            slabs,
            pltpu.VMEM((devices * SUB, 2 * LANES), f32),
            pltpu.VMEM((halves, devices * SUB, 2 * LANES), f32),
            pltpu.VMEM((devices * SUB, 2 * LANES), f32),
            pltpu.SemaphoreType.DMA((len(operands),)),
            pltpu.SemaphoreType.DMA((2,)),
            pltpu.SemaphoreType.DMA((3, max(halves, 2))),
            pltpu.SemaphoreType.DMA((3, max(halves, 2))),
        ],
        compiler_params=pltpu.CompilerParams(collective_id=0, has_side_effects=True),
    )(*operands)


def on_device(groups, shards, projections, short_taps, long_filter, skip_gain):
    _, positions, channels = projections.shape
    devices = groups * shards
    fits = (
        positions == LANES
        and channels % LANES == 0
        and channels % (SUB * devices) == 0
        and LANES % (channels // devices) == 0
        and devices & (devices - 1) == 0
        and (channels // devices) % 16 == 0
        and devices % TOGETHER == 0
        and short_taps.shape[1] <= HALO
    )
    if not fits:
        return per_device(projections, short_taps, long_filter, skip_gain)
    consts = tables(devices, positions)
    return owned_channels(consts, groups, shards, projections, short_taps, long_filter, skip_gain)


def solution(mesh):
    placed = (P(None, ("grp", "shard"), None), P(), P(("grp", "shard"), None), P())
    body = functools.partial(on_device, mesh.shape["grp"], mesh.shape["shard"])
    return jax.shard_map(
        body, mesh=mesh, in_specs=placed, out_specs=P(("grp", "shard"), None), check_vma=False
    )
```
